32 devices in a mesh: row: 4 (over y, x), col: 8 (over z, core).
Axes of the slice: x: 2, y: 2, z: 4, core: 2. Of those that a mesh axis runs over, the one named last changes fastest.
Arguments:
- query_act: bfloat16 [768, 16384], P(None, 'row'), may hold values from -6 to 6
- query_grad: bfloat16 [768, 16384], P(None, 'col'), may hold values from -6 to 6
- train_rot: bfloat16 [384, 16384], P(None, 'col'), may hold values from -6 to 6
- basis_in: bfloat16 [16384, 16384], P('row', 'col'), may hold values from -0.046875 to 0.046875
- basis_out: bfloat16 [16384, 16384], P('col', 'row'), may hold values from -0.046875 to 0.046875
- eig_in: float32 [16384], replicated, may hold values from 0.05 to 2
- eig_out: float32 [16384], replicated, may hold values from 0.05 to 2
Outputs:
- predicted: float32 [384, 16384], P('row', 'col')
The draws below stay inside these ranges and needn't reach their ends.
All inputs are finite; a program needn't handle non-finite values.
Results may differ from the reference program's by a relative error of at most 0.0049.
Values may be sent and summed in bfloat16 or wider, within the bound.
A program may use at most 128 MiB of HBM per device.

```python
import math
import jax
import jax.numpy as jnp
from jax import lax

DI = 16384
DO = 16384
QUERIES = 768
TRAIN = 384


def steps_of(key, extent, split, low, high):
    level = 1.0
    for dim, parts in split:
        steps = jax.random.uniform(jax.random.fold_in(jax.random.fold_in(key, 6), dim), (parts,), jnp.float32, low / len(split), high / len(split))
        level = level * jnp.repeat(jnp.exp(steps), extent[dim] // parts).reshape((-1,) + (1,) * (len(extent) - 1 - dim))
    return level


def scatter_about(own_key, dims, width, reach, shards=(), kind=jnp.bfloat16):
    result = jax.random.normal(own_key, dims, jnp.float32) * width
    if len(shards) > 0:
        result = steps_of(own_key, dims, shards, -0.22, 0.18) * result
    return jnp.clip(result, min=-reach, max=reach).astype(kind)


def setup_inputs(seed: int = 0) -> dict:
    keys = jax.random.split(jax.random.key(seed), 8)
    return {
        "query_act": scatter_about(keys[0], (QUERIES, DI), 1.0, 6.0, ((1, 4),)),
        "query_grad": scatter_about(keys[1], (QUERIES, DO), 1.0, 6.0, ((1, 8),)),
        "train_rot": scatter_about(keys[2], (TRAIN, DI), 1.0, 6.0, ((1, 8),)),
        "basis_in": scatter_about(keys[3], (DI, DI), DI ** -0.5, 0.046875, ((0, 4), (1, 8))),
        "basis_out": scatter_about(keys[4], (DO, DO), DO ** -0.5, 0.046875, ((0, 8), (1, 4))),
        "eig_in": jnp.clip(jnp.exp(jax.random.uniform(keys[5], (DI,), jnp.float32, math.log(0.05), math.log(2.0))), 0.05, 2.0),
        "eig_out": jnp.clip(jnp.exp(jax.random.uniform(keys[6], (DO,), jnp.float32, math.log(0.05), math.log(2.0))), 0.05, 2.0),
    }


damping_share = 0.1

def math_sqrt(value):
    return float(value) ** 0.5

def reference(query_act, query_grad, train_rot, basis_in, basis_out, eig_in, eig_out):
    act_rot = jnp.dot(query_act, basis_in, preferred_element_type=jnp.float32).astype(jnp.bfloat16)
    grad_rot = jnp.dot(query_grad, basis_out, preferred_element_type=jnp.float32).astype(jnp.bfloat16)
    damp = damping_share * jnp.mean(eig_in) * jnp.mean(eig_out)
    block = min(DO, 1024)
    count = DO // block

    def one_block(index):
        start = (index * block).astype(jnp.int32)
        grad_part = lax.dynamic_slice_in_dim(grad_rot, start, block, 1)
        eig_part = lax.dynamic_slice_in_dim(eig_out, start, block, 0)
        outer = lax.dot_general(grad_part, act_rot, (((0,), (0,)), ((), ())), preferred_element_type=jnp.float32)
        scaled = (outer / QUERIES / (eig_part[:, None] * eig_in[None, :] + damp)).astype(jnp.bfloat16)
        return lax.dot_general(train_rot, scaled, (((1,), (1,)), ((), ())), preferred_element_type=jnp.float32)
    pieces = lax.map(one_block, jnp.arange(count, dtype=jnp.int32))
    inner = jnp.transpose(pieces, (1, 0, 2)).reshape(TRAIN, DO)
    inner = (inner * (1.0 / math_sqrt(DI))).astype(jnp.bfloat16)
    return lax.dot_general(inner, basis_out, (((1,), (1,)), ((), ())), preferred_element_type=jnp.float32)
```

```python
import jax
import jax.numpy as jnp
from jax import lax
from jax.sharding import PartitionSpec as P

damping_share = 0.1
num_chunks = 2


def shifted(size, step, stride=1):
    group = size // stride
    return [(i, (i // stride + step) % group * stride + i % stride) for i in range(size)]


def exchange_sum(part, axis, stride=1):
    size = lax.axis_size(axis)
    group = size // stride
    me = lax.axis_index(axis) // stride
    rows = part.shape[0] // group

    def block_of(owner):
        return lax.dynamic_slice_in_dim(part, owner * rows, rows, 0)

    received = [
        lax.ppermute(
            block_of((me + step) % group).astype(jnp.bfloat16), axis, shifted(size, step, stride)
        )
        for step in range(1, group)
    ]
    total = block_of(me)
    for block in received:
        total = total + block.astype(jnp.float32)
    return total


def pair_exchange_sum(part, axis):
    size = lax.axis_size(axis)
    side = lax.axis_index(axis) % 2
    rows = part.shape[0] // size
    blocks = part.reshape(size // 2, 2, rows, part.shape[1])

    def half(which):
        taken = lax.dynamic_slice_in_dim(blocks, which, 1, 1)
        return taken.reshape(size // 2 * rows, part.shape[1])

    got = lax.ppermute(half(1 - side), axis, [(i, i ^ 1) for i in range(size)])
    return exchange_sum(half(side) + got, axis, 2)


def exchange_gather(piece, axis):
    size = lax.axis_size(axis)
    me = lax.axis_index(axis)
    rows = piece.shape[0]
    pieces = [(me, piece)]
    for step in range(1, size):
        pieces.append(((me - step) % size, lax.ppermute(piece, axis, shifted(size, step))))
    whole = jnp.zeros((size * rows, piece.shape[1]), piece.dtype)
    for owner, block in pieces:
        whole = lax.dynamic_update_slice_in_dim(whole, block, owner * rows, 0)
    return whole


def per_device(query_act, query_grad, train_rot, basis_in, basis_out, eig_in, eig_out):
    width_in = eig_in.shape[0]
    out_rows = basis_out.shape[1]
    in_cols = basis_in.shape[1]
    num_queries = query_act.shape[0]
    chunk = out_rows // num_chunks
    basis_chunks = [basis_out[:, k * chunk : (k + 1) * chunk] for k in range(num_chunks)]

    grad_pieces = []
    for basis in basis_chunks:
        grad_part = jnp.dot(query_grad, basis, preferred_element_type=jnp.float32)
        grad_pieces.append(pair_exchange_sum(grad_part, "col").astype(jnp.bfloat16))
    act_part = jnp.dot(query_act, basis_in, preferred_element_type=jnp.float32)
    grad_pieces = [lax.optimization_barrier((piece, act_part))[0] for piece in grad_pieces]
    act_piece = exchange_sum(act_part, "row").astype(jnp.bfloat16)
    act_rot = exchange_gather(act_piece, "row")
    grad_rots = [lax.all_gather(piece, "col", axis=0, tiled=True) for piece in grad_pieces]

    damp = damping_share * jnp.mean(eig_in) * jnp.mean(eig_out) * num_queries
    out_start = lax.axis_index("row") * out_rows
    in_start = lax.axis_index("col") * in_cols
    eig_out_part = lax.dynamic_slice_in_dim(eig_out, out_start, out_rows, 0) * num_queries
    eig_in_part = lax.dynamic_slice_in_dim(eig_in, in_start, in_cols, 0)
    factor = 1.0 / float(width_in) ** 0.5

    inner_pieces = []
    for k in range(num_chunks):
        outer = lax.dot_general(
            grad_rots[k], act_rot, (((0,), (0,)), ((), ())), preferred_element_type=jnp.float32
        )
        eig_chunk = eig_out_part[k * chunk : (k + 1) * chunk]
        scaled = (outer / (eig_chunk[:, None] * eig_in_part[None, :] + damp)).astype(jnp.bfloat16)
        partial_inner = lax.dot_general(
            train_rot, scaled, (((1,), (1,)), ((), ())), preferred_element_type=jnp.float32
        )
        inner_pieces.append((pair_exchange_sum(partial_inner, "col") * factor).astype(jnp.bfloat16))
    partial_out = None
    for k in range(num_chunks):
        inner = lax.all_gather(inner_pieces[k], "col", axis=0, tiled=True)
        term = lax.dot_general(
            inner, basis_chunks[k], (((1,), (1,)), ((), ())), preferred_element_type=jnp.float32
        )
        partial_out = term if partial_out is None else partial_out + term
    return exchange_sum(partial_out, "row")


def solution(mesh):
    in_specs = (
        P(None, "row"),
        P(None, "col"),
        P(None, "col"),
        P("row", "col"),
        P("col", "row"),
        P(),
        P(),
    )
    out_specs = P("row", "col")
    return jax.shard_map(
        per_device, mesh=mesh, in_specs=in_specs, out_specs=out_specs, check_vma=False
    )
```
